256 devices in a mesh: param: 64 (over x, z, core), ex: 4 (over y).
Axes of the slice: x: 4, y: 4, z: 8, core: 2. Of those that a mesh axis runs over, the one named last changes fastest.
Arguments:
- gradients: float32 [256, 262144], P('ex', 'param')
- m_state: float32 [262144], P('param'), may hold values from -0.6 to 0.6
- v_state: float32 [262144], P('param'), may hold values from 0.001 to 0.1
- row_seeds: int32 [262144], P('param'), may hold values from 1 to 2999999
- col_seeds: int32 [8192], replicated, may hold values from 1 to 2999999
- group_of: int32 [256], replicated, may hold values from 0 to 56, as said below
Outputs:
- features: float32 [256, 8192], P('ex', 'param')
- scores: float32 [256, 57], P('ex')
The draws below stay inside these ranges and needn't reach their ends.
Inputs may be any that keep to these rules, and one draw needn't show every extreme that they name: `group_of`: every one of the 57 subtasks holds at least one example.
All inputs are finite; a program needn't handle non-finite values.
Results may differ from the reference program's by a relative error of at most 0.0029.
Values sent between devices are 32-bit elements; how exact they have to be, the bound alone decides.
A program may use at most 64 MiB of HBM per device.

```python
import math
import jax
import jax.numpy as jnp
from jax import lax

K = 8192
GROUPS = 57
EXAMPLES = 256
PARAMS = 262144


def draw_gradients(key, part):
    scale_key = jax.random.fold_in(key, 11)
    noise_key = jax.random.fold_in(key, 12)
    scales = jnp.exp(jax.random.uniform(scale_key, (EXAMPLES, 1), jnp.float32, jnp.log(0.3), jnp.log(3.0)))
    noise = jax.random.normal(noise_key, (EXAMPLES, PARAMS), jnp.float32)
    return noise * scales


def draw_group_of(key, part):
    rest_key = jax.random.fold_in(key, 21)
    order_key = jax.random.fold_in(key, 22)
    rest = jax.random.randint(rest_key, (EXAMPLES - GROUPS,), 0, GROUPS, jnp.int32)
    labels = jnp.concatenate([jnp.arange(GROUPS, dtype=jnp.int32), rest])
    return jax.random.permutation(order_key, labels)


def plant(entries, stream_key, least, largest):
    longest = entries.shape.index(max(entries.shape))
    spots = []
    for shift in (0, 1):
        where = [jax.random.randint(jax.random.fold_in(stream_key, axis), (), 0, length) for axis, length in enumerate(entries.shape)]
        where[longest] = (where[longest] + shift) % entries.shape[longest]
        spots.append(tuple(where))
    return entries.at[spots[0]].set(least).at[spots[1]].set(largest)


def steps_of(stream_key, dims, shards, least, largest):
    gain = 1.0
    for axis_at, blocks in shards:
        draws = jax.random.uniform(jax.random.fold_in(jax.random.fold_in(stream_key, 6), axis_at), (blocks,), jnp.float32, least / len(shards), largest / len(shards))
        gain = gain * jnp.repeat(jnp.exp(draws), dims[axis_at] // blocks).reshape((-1,) + (1,) * (len(dims) - 1 - axis_at))
    return gain


def centred(key, shape, deviation, limit, shards=(), kind=jnp.bfloat16):
    drawn = deviation * jax.random.normal(key, shape, jnp.float32)
    if shards:
        drawn = drawn * steps_of(key, shape, shards, -0.22, 0.18)
    return jnp.clip(drawn, -limit, limit).astype(kind)


def setup_inputs(seed: int = 0) -> dict:
    keys = jax.random.split(jax.random.key(seed), 7)
    gradients = draw_gradients(jax.random.fold_in(keys[6], 71), 0)
    m_state = centred(keys[1], (PARAMS,), 0.1, 0.6, ((0, 64),), jnp.float32)
    v_state = jnp.clip(jnp.exp(math.log(0.1) - 4.6051702 * jax.random.uniform(keys[2], (PARAMS,), jnp.float32) ** steps_of(keys[2], (PARAMS,), ((0, 64),), -0.2, 0.2)), 0.001, 0.1)
    row_seeds = plant(jax.random.randint(keys[3], (PARAMS,), 1, 3000000), jax.random.fold_in(keys[3], 1), 1, 2999999).astype(jnp.int32)
    col_seeds = plant(jax.random.randint(keys[4], (K,), 1, 3000000), jax.random.fold_in(keys[4], 1), 1, 2999999).astype(jnp.int32)
    group_of = draw_group_of(jax.random.fold_in(keys[6], 71), 0)
    return dict(gradients=gradients, m_state=m_state, v_state=v_state, row_seeds=row_seeds, col_seeds=col_seeds, group_of=group_of)


def hashed_signs(row_part, col_part):
    hashed = row_part[:, None] * col_part[None, :]
    hashed = hashed ^ hashed >> 15
    hashed = hashed * jnp.int32(739982445)
    hashed = hashed ^ hashed >> 13
    return (1 - 2 * (hashed >> 11 & 1)).astype(jnp.bfloat16)

def reference(gradients, m_state, v_state, row_seeds, col_seeds, group_of):
    first_moment = 0.9 * m_state[None, :] + 0.1 * gradients
    second_moment = 0.999 * v_state[None, :] + 0.001 * gradients * gradients
    update = (first_moment / (jnp.sqrt(second_moment) + 1e-08)).astype(jnp.bfloat16)
    block_width = min(4096, PARAMS)
    blocks = PARAMS // block_width

    def accumulate(summed, block_index):
        begin_at = (block_index * block_width).astype(jnp.int32)
        seed_rows = lax.dynamic_slice_in_dim(row_seeds, begin_at, block_width)
        columns = lax.dynamic_slice_in_dim(update, begin_at, block_width, 1)
        return (summed + jnp.dot(columns, hashed_signs(seed_rows, col_seeds), preferred_element_type=jnp.float32), None)
    projected, unused = lax.scan(accumulate, jnp.zeros((EXAMPLES, K), jnp.float32), jnp.arange(blocks, dtype=jnp.int32))
    root_mean = jnp.sqrt(lax.optimization_barrier(jnp.mean(projected * projected, axis=1, keepdims=True)) + 1e-06)
    features = projected / root_mean
    products = jnp.dot(features, features.T, precision=lax.Precision.HIGHEST)
    onehot = (group_of[:, None] == jnp.arange(GROUPS, dtype=jnp.int32)[None, :]).astype(jnp.float32)
    counts = lax.optimization_barrier(jnp.sum(onehot, axis=0))
    scores = jnp.dot(products, onehot, precision=lax.Precision.HIGHEST) / (counts[None, :] * K)
    return (features, scores)
```

```python
import functools

import jax
import jax.numpy as jnp
from jax import lax
from jax.experimental import pallas as pl
from jax.experimental.pallas import tpu as pltpu
from jax.sharding import PartitionSpec as P

GROUPS = 57
X, Z, C, Y = 4, 8, 2, 4
XC = X * C
LANES = 128
ALONE = 8
MESH = pl.DeviceIdType.MESH
HIGH = lax.Precision.HIGHEST
F32 = jnp.float32

FACTOR = (739982445 << 4) & 0xFFFFFFFF
FACTOR = FACTOR - (1 << 32) if FACTOR >= 1 << 31 else FACTOR


def signs_of(product):
    mixed = product ^ (product >> 15)
    mixed = mixed * jnp.int32(FACTOR)
    mixed = mixed ^ (mixed >> 13)
    return jnp.where(mixed.astype(jnp.int16) < jnp.int16(0), jnp.bfloat16(-1), jnp.bfloat16(1))


def update_of(grad, mean, square):
    first = 0.9 * mean + 0.1 * grad
    second = 0.999 * square + 0.001 * grad * grad
    return (first / (jnp.sqrt(second) + 1e-08)).astype(jnp.bfloat16)


def contract(a, b):
    return lax.dot_general(a, b, (((1,), (1,)), ((), ())), precision=HIGH, preferred_element_type=F32)


def kernel(
    g_ref, m_ref, v_ref, r_ref, k_ref, group_ref,
    f_ref, s_ref,
    u_own, seeds,
    part_a, chip_a, sum_a, cols_a, rows_a, got_a,
    ybuf, send1, recv1, send2, recv2, out1, out2,
    cs_a, cr_a, xs_a, xr_a, zs_a, zr_a,
    ys, yr, s1s, s1r, s2s, s2r, o1s, o1r, o2s, o2r,
):
    me, y = lax.axis_index("param"), lax.axis_index("ex")
    x, z, c = me // (Z * C), (me // C) % Z, me % C
    xc = x * C + c
    examples, params = g_ref.shape
    features = k_ref.shape[0] * LANES

    def at(x_to, z_to, c_to):
        return ((x_to * Z + z_to) * C + c_to, y)

    def at_xc(to):
        return at(to // C, z, to % C)

    def send(src, dst, send_sem, recv_sem, device):
        return pltpu.make_async_remote_copy(
            src_ref=src, dst_ref=dst, send_sem=send_sem, recv_sem=recv_sem,
            device_id=device, device_id_type=MESH,
        )

    barrier = pltpu.get_barrier_semaphore()

    def greet(device):
        pl.semaphore_signal(barrier, inc=1, device_id=device, device_id_type=MESH)

    for d in range(1, XC):
        greet(at_xc((xc + d) % XC))
    for d in range(1, Z):
        greet(at(x, (z + d) % Z, c))
    for d in range(1, Y):
        greet((me, (y + d) % Y))

    def prepare(i, carry):
        lanes = pl.ds(pl.multiple_of(i * LANES, LANES), LANES)
        u_own[:, lanes] = update_of(g_ref[:, lanes], m_ref[pl.ds(i, 1), :], v_ref[pl.ds(i, 1), :])
        seeds[lanes, :] = jnp.broadcast_to(r_ref[pl.ds(i, 1), :], (LANES, LANES)).T
        return carry

    lax.fori_loop(0, params // LANES, prepare, 0)
    pl.semaphore_wait(barrier, (XC - 1) + (Z - 1) + (Y - 1))

    def place(t):
        return (x + 1 + t % X) % X, (z + 1 + t // X) % Z

    def chunk(update, depth, base, t):
        x_to, z_to = place(t)
        row = (x_to * Z + z_to) * C
        left, right = k_ref[pl.ds(row, 1), :], k_ref[pl.ds(row + 1, 1), :]
        strips = []
        for p in range(0, depth, 16):
            seed = seeds[pl.ds(pl.multiple_of(base + p, 16), 16), :]
            strips.append(jnp.concatenate([signs_of(seed * left), signs_of(seed * right)], axis=1))
        return jnp.dot(update, jnp.concatenate(strips, axis=0), preferred_element_type=F32)

    def chip_copy(t):
        return send(part_a.at[t, 1 - c], chip_a.at[t], cs_a.at[t], cr_a.at[t], at(x, z, 1 - c))

    def x_copy(t):
        slot = t // X, t % X
        return send(sum_a.at[slot], cols_a.at[slot], xs_a.at[slot], xr_a.at[slot], at((x + 1 + t % X) % X, z, c))

    def z_copy(group):
        return send(rows_a.at[group], got_a.at[group], zs_a.at[group], zr_a.at[group], at(x, (z + 1 + group) % Z, c))

    def after_chip(t):
        chip_copy(t).wait_recv()
        sum_a[t // X, t % X] = part_a[t, c] + chip_a[t]

        @pl.when(t % X < X - 1)
        def _():
            x_copy(t).start()

    def after_x(group):
        for j in range(X - 1):
            x_copy(group * X + j).wait_recv()
        rows_a[group] = sum_a[group, X - 1] + cols_a[group, 0] + cols_a[group, 1] + cols_a[group, 2]

    def step(t, carry):
        part = chunk(u_own[...], params, 0, t)
        part_a[t, 0] = part[:, :LANES]
        part_a[t, 1] = part[:, LANES:]
        chip_copy(t).start()

        @pl.when(t >= 1)
        def _():
            after_chip(t - 1)

        @pl.when((t % X == 2) & (t > X))
        def _():
            after_x(t // X - 1)
            z_copy(t // X - 1).start()

        return carry

    lax.fori_loop(0, Z * X, step, 0)
    after_chip(Z * X - 1)
    after_x(Z - 1)
    total = rows_a[Z - 1]
    for group in range(Z - 1):
        z_copy(group).wait_recv()
        total = total + got_a[group]

    ybuf[y] = total

    def y_copy(d):
        return send(ybuf.at[y], ybuf.at[y], ys.at[d - 1], yr.at[d - 1], (me, (y + d) % Y))

    for d in range(1, Y):
        y_copy(d).start()
    for d in range(1, Y):
        y_copy(d).wait_recv()
    every = ybuf[...].reshape(Y * examples, LANES)

    products = contract(total, every)
    squares = contract(jnp.ones((8, LANES), F32), every * every)
    send1[...] = jnp.zeros_like(send1)
    for j in range(Z):
        send1[j, :, : Y * examples] = products[j * XC : (j + 1) * XC, :]
        for h in range(2):
            send1[j, h : h + 1, Y * examples :] = squares[:1, h * LANES : (h + 1) * LANES]

    def send1_copy(d):
        to = (z + d) % Z
        return send(send1.at[to], recv1.at[d - 1], s1s.at[d - 1], s1r.at[d - 1], at(x, to, c))

    for d in range(1, Z):
        send1_copy(d).start()
    block = send1[z]
    for d in range(1, Z):
        send1_copy(d).wait_recv()
        block = block + recv1[d - 1]

    for j in range(XC):
        for h in range(2):
            send2[j, h : h + 1, :] = block[j : j + 1, h * LANES : (h + 1) * LANES]
            send2[j, 2 + h : 3 + h, :] = block[h : h + 1, Y * examples :]

    def send2_copy(d):
        to = (xc + d) % XC
        return send(send2.at[to], recv2.at[d - 1], s2s.at[d - 1], s2r.at[d - 1], at_xc(to))

    for d in range(1, XC):
        send2_copy(d).start()
    mine = send2[xc]
    for d in range(1, XC):
        send2_copy(d).wait_recv()
        mine = mine + recv2[d - 1]

    root_mean = jnp.sqrt(mine[2:4, :] / features + 1e-06)
    weights = mine[0:2, :] / root_mean
    example = y * examples + z * XC + xc
    places = LANES * lax.broadcasted_iota(jnp.int32, (2, LANES), 0) + lax.broadcasted_iota(jnp.int32, (2, LANES), 1)
    own_root = jnp.sum(jnp.where(places == example, root_mean, 0.0), keepdims=True)
    score, count = jnp.zeros((8, LANES), F32), jnp.zeros((8, LANES), F32)
    for h in range(2):
        labels = lax.broadcasted_iota(jnp.int32, (LANES, LANES), 0)
        onehot = (labels == group_ref[h : h + 1, :]).astype(F32)
        score = score + contract(jnp.broadcast_to(weights[h : h + 1, :], (8, LANES)), onehot)
        count = count + contract(jnp.ones((8, LANES), F32), onehot)
    count = jnp.where(count == 0, 1.0, count)
    out1[xc] = (score / own_root / (count * features))[:1, :]

    def out1_copy(d):
        return send(out1.at[xc], out1.at[xc], o1s.at[d - 1], o1r.at[d - 1], at_xc((xc + d) % XC))

    for d in range(1, XC):
        out1_copy(d).start()

    here = y * examples + lax.broadcasted_iota(jnp.int32, (examples, LANES), 0)
    lane = lax.broadcasted_iota(jnp.int32, (examples, LANES), 1)
    column = jnp.zeros((examples, 1), F32)
    for h in range(2):
        row = jnp.broadcast_to(root_mean[h : h + 1, :], (examples, LANES))
        column = column + jnp.sum(jnp.where(lane + h * LANES == here, row, 0.0), axis=1, keepdims=True)
    f_ref[...] = total / column

    for d in range(1, XC):
        out1_copy(d).wait_recv()
    out2[z] = out1[...]

    def out2_copy(d):
        return send(out1, out2.at[z], o2s.at[d - 1], o2r.at[d - 1], at(x, (z + d) % Z, c))

    for d in range(1, Z):
        out2_copy(d).start()
    for d in range(1, Z):
        out2_copy(d).wait_recv()
    for j in range(Z):
        for i in range(XC):
            s_ref[j * XC + i : j * XC + i + 1, :] = out2[j, i][:, :GROUPS]

    def chip_sent(t, carry):
        chip_copy(t).wait_send()

        @pl.when(t % X < X - 1)
        def _():
            x_copy(t).wait_send()

        return carry

    lax.fori_loop(0, Z * X, chip_sent, 0)
    for group in range(Z - 1):
        z_copy(group).wait_send()
    for d in range(1, Y):
        y_copy(d).wait_send()
    for d in range(1, Z):
        send1_copy(d).wait_send()
        out2_copy(d).wait_send()
    for d in range(1, XC):
        send2_copy(d).wait_send()
        out1_copy(d).wait_send()


def solution(mesh):
    def shards(gradients, m_state, v_state, row_seeds, col_seeds, group_of):
        examples, params = gradients.shape
        rows = (-1, LANES)
        dma, vmem = pltpu.SemaphoreType.DMA, pltpu.VMEM
        steps = Z * X
        block = (examples, LANES)
        wide = (Y * examples) + LANES
        return pl.pallas_call(
            kernel,
            out_shape=(
                jax.ShapeDtypeStruct((examples, LANES), F32),
                jax.ShapeDtypeStruct((examples, GROUPS), F32),
            ),
            in_specs=[pl.BlockSpec(memory_space=pltpu.VMEM)] * 6,
            out_specs=[pl.BlockSpec(memory_space=pltpu.VMEM)] * 2,
            scratch_shapes=[
                vmem((examples, params), jnp.bfloat16),
                vmem((params, LANES), jnp.int32),
                vmem((steps, 2, *block), F32),
                vmem((steps, *block), F32),
                vmem((Z, X, *block), F32),
                vmem((Z, X, *block), F32),
                vmem((Z, *block), F32),
                vmem((Z, *block), F32),
                vmem((Y, *block), F32),
                vmem((Z, XC, wide), F32),
                vmem((Z - 1, XC, wide), F32),
                vmem((XC, 4, LANES), F32),
                vmem((XC - 1, 4, LANES), F32),
                vmem((XC, 1, LANES), F32),
                vmem((Z, XC, 1, LANES), F32),
                dma((steps,)), dma((steps,)),
                dma((Z, X)), dma((Z, X)),
                dma((Z,)), dma((Z,)),
                dma((Y - 1,)), dma((Y - 1,)),
                dma((Z - 1,)), dma((Z - 1,)),
                dma((XC - 1,)), dma((XC - 1,)),
                dma((XC - 1,)), dma((XC - 1,)),
                dma((Z - 1,)), dma((Z - 1,)),
            ],
            compiler_params=pltpu.CompilerParams(
                collective_id=0, has_side_effects=True, vmem_limit_bytes=48 << 20
            ),
            name="features_and_scores",
        )(
            gradients, m_state.reshape(rows), v_state.reshape(rows), row_seeds.reshape(rows),
            col_seeds.reshape(rows), group_of.reshape(rows),
        )

    in_specs = (P("ex", "param"), P("param"), P("param"), P("param"), P(), P())
    out_specs = (P("ex", "param"), P("ex", None))
    return jax.shard_map(shards, mesh=mesh, in_specs=in_specs, out_specs=out_specs, check_vma=False)
```

```python
import functools

import jax
import jax.numpy as jnp
from jax import lax
from jax.experimental import pallas as pl
from jax.experimental.pallas import tpu as pltpu
from jax.sharding import PartitionSpec as P

GROUPS = 57
X, Z, C, Y = 4, 8, 2, 4
XC = X * C
LANES = 128
ALONE = 3
LATE = 3
LAST = Z * X - 1
FARTHEST_FIRST = (4, 3, 5, 2, 6, 1, 7)
MESH = pl.DeviceIdType.MESH
HIGH = lax.Precision.HIGHEST
F32 = jnp.float32

FACTOR = (739982445 << 4) & 0xFFFFFFFF
FACTOR = FACTOR - (1 << 32) if FACTOR >= 1 << 31 else FACTOR


def signs_of(product):
    mixed = product ^ (product >> 15)
    mixed = mixed * jnp.int32(FACTOR)
    mixed = mixed ^ (mixed >> 13)
    return jnp.where(mixed.astype(jnp.int16) < jnp.int16(0), jnp.bfloat16(-1), jnp.bfloat16(1))


def update_of(grad, mean, square):
    first = 0.9 * mean + 0.1 * grad
    second = 0.999 * square + 0.001 * grad * grad
    return (first / (jnp.sqrt(second) + 1e-08)).astype(jnp.bfloat16)


def contract(a, b):
    return lax.dot_general(a, b, (((1,), (1,)), ((), ())), precision=HIGH, preferred_element_type=F32)


def remote(src, dst, send_sem, recv_sem, device):
    return pltpu.make_async_remote_copy(
        src_ref=src, dst_ref=dst, send_sem=send_sem, recv_sem=recv_sem,
        device_id=device, device_id_type=MESH,
    )


class Sums:
    def __init__(self, begin, at, x, z, c, buffers, semaphores):
        self.begin, self.at, self.x, self.z, self.c = begin, at, x, z, c
        self.part, self.chip, self.sum, self.cols, self.rows, self.got = buffers
        self.cs, self.cr, self.xs, self.xr, self.zs, self.zr = semaphores

    def slot(self, t):
        return t // X - self.begin, t % X

    def put(self, t, value):
        i = t - self.begin * X
        self.part[i, 0] = value[:, :LANES]
        self.part[i, 1] = value[:, LANES:]

    def chip_copy(self, t):
        i = t - self.begin * X
        return remote(
            self.part.at[i, 1 - self.c], self.chip.at[i], self.cs.at[i], self.cr.at[i],
            self.at(self.x, self.z, 1 - self.c),
        )

    def x_copy(self, t):
        i = self.slot(t)
        to = self.at((self.x + 1 + t % X) % X, self.z, self.c)
        return remote(self.sum.at[i], self.cols.at[i], self.xs.at[i], self.xr.at[i], to)

    def z_copy(self, group):
        i = group - self.begin
        to = self.at(self.x, (self.z + 1 + group) % Z, self.c)
        return remote(self.rows.at[i], self.got.at[i], self.zs.at[i], self.zr.at[i], to)

    def after_chip(self, t):
        i = t - self.begin * X
        self.chip_copy(t).wait_recv()
        self.sum[self.slot(t)] = self.part[i, self.c] + self.chip[i]

        @pl.when(t % X < X - 1)
        def _():
            self.x_copy(t).start()

    def after_x(self, group):
        i = group - self.begin
        for j in range(X - 1):
            self.x_copy(group * X + j).wait_recv()
        self.rows[i] = self.sum[i, X - 1] + self.cols[i, 0] + self.cols[i, 1] + self.cols[i, 2]

    def sent(self, end):
        def one(t, carry):
            self.chip_copy(t).wait_send()

            @pl.when(t % X < X - 1)
            def _():
                self.x_copy(t).wait_send()

            return carry

        lax.fori_loop(self.begin * X, end * X, one, 0)
        for group in range(self.begin, min(end, Z - 1)):
            self.z_copy(group).wait_send()


def kernel(
    g_in, m_in, v_in, r_in, k_in, group_in,
    f_ref, s_ref,
    g_ref, m_ref, v_ref, r_ref, k_ref, group_ref, in_sems,
    u_own, u_both, g_other, seeds,
    part_a, chip_a, sum_a, cols_a, rows_a, got_a,
    part_b, chip_b, sum_b, cols_b, rows_b, got_b,
    ybuf, blocks, send1, recv1, planes, scored,
    gs, gr,
    cs_a, cr_a, xs_a, xr_a, zs_a, zr_a,
    cs_b, cr_b, xs_b, xr_b, zs_b, zr_b,
    ys, yr, s1s, s1r, s2s, s2r, o1s, o1r,
):
    me, y = lax.axis_index("param"), lax.axis_index("ex")
    x, z, c = me // (Z * C), (me // C) % Z, me % C
    xc = x * C + c
    side = y % 2
    partner = (me, y + 1 - 2 * side)
    examples, params = g_ref.shape
    half = params // 2
    features = k_ref.shape[0] * LANES
    send = remote

    inputs = [
        pltpu.make_async_copy(src, dst, in_sems.at[i])
        for i, (src, dst) in enumerate(
            [(g_in, g_ref), (m_in, m_ref), (v_in, v_ref), (r_in, r_ref), (k_in, k_ref), (group_in, group_ref)]
        )
    ]
    for copy in inputs:
        copy.start()

    def at(x_to, z_to, c_to):
        return ((x_to * Z + z_to) * C + c_to, y)

    def at_xc(to):
        return at(to // C, z, to % C)

    barrier = pltpu.get_barrier_semaphore()

    def greet(device):
        pl.semaphore_signal(barrier, inc=1, device_id=device, device_id_type=MESH)

    for d in FARTHEST_FIRST:
        greet(at(x, (z + d) % Z, c))
    for d in range(1, XC):
        greet(at_xc((xc + d) % XC))
    for d in range(1, Y):
        greet((me, (y + d) % Y))
    for copy in inputs:
        copy.wait()

    def prepare(i, carry):
        for k in range(4):
            row = i * 4 + k
            lanes = pl.ds(pl.multiple_of(row * LANES, LANES), LANES)
            u_own[:, lanes] = update_of(g_ref[:, lanes], m_ref[pl.ds(row, 1), :], v_ref[pl.ds(row, 1), :])
            seeds[lanes, :] = jnp.broadcast_to(r_ref[pl.ds(row, 1), :], (LANES, LANES)).T
        return carry

    lax.fori_loop(0, params // LANES // 4, prepare, 0)

    def chunk(update, depth, base, t):
        x_to, z_to = (x + 1 + t % X) % X, (z + 1 + t // X) % Z
        row = (x_to * Z + z_to) * C
        left, right = k_ref[pl.ds(row, 1), :], k_ref[pl.ds(row + 1, 1), :]
        strips = []
        for p in range(0, depth, 16):
            seed = seeds[pl.ds(pl.multiple_of(base + p, 16), 16), :]
            strips.append(jnp.concatenate([signs_of(seed * left), signs_of(seed * right)], axis=1))
        return jnp.dot(update, jnp.concatenate(strips, axis=0), preferred_element_type=F32)

    alone = Sums(
        0, at, x, z, c,
        (part_a, chip_a, sum_a, cols_a, rows_a, got_a), (cs_a, cr_a, xs_a, xr_a, zs_a, zr_a),
    )
    both = Sums(
        ALONE, at, x, z, c,
        (part_b, chip_b, sum_b, cols_b, rows_b, got_b), (cs_b, cr_b, xs_b, xr_b, zs_b, zr_b),
    )
    exchange = send(
        g_ref.at[:, pl.ds(pl.multiple_of((1 - side) * half, half), half)], g_other, gs.at[0], gr.at[0], partner
    )

    def early(t, carry):
        alone.put(t, chunk(u_own[...], params, 0, t))
        return carry

    def step_alone(t, carry):
        early(t, carry)
        alone.chip_copy(t).start()

        @pl.when(t == LATE + 1)
        def _():
            for i in range(LATE):
                alone.after_chip(i)

        alone.after_chip(t - 1)

        @pl.when((t % X == 2) & (t >= X + 2))
        def _():
            alone.after_x(t // X - 1)
            alone.z_copy(t // X - 1).start()

        return carry

    lax.fori_loop(0, LATE + 1, early, 0)
    pl.semaphore_wait(barrier, (XC - 1) + (Z - 1) + (Y - 1))
    exchange.start()
    for t in range(LATE + 1):
        alone.chip_copy(t).start()
    lax.fori_loop(LATE + 1, ALONE * X, step_alone, 0)

    u_both[side] = u_own[:, pl.ds(pl.multiple_of(side * half, half), half)]
    exchange.wait_recv()

    def prepare_other(i, carry):
        for k in range(4):
            lanes = pl.ds(pl.multiple_of((i * 4 + k) * LANES, LANES), LANES)
            row = side * (half // LANES) + i * 4 + k
            u_both[1 - side, :, lanes] = update_of(g_other[:, lanes], m_ref[pl.ds(row, 1), :], v_ref[pl.ds(row, 1), :])
        return carry

    lax.fori_loop(0, half // LANES // 4, prepare_other, 0)

    def step_both(t, carry):
        both.put(t, chunk(u_both[...].reshape(2 * examples, half), half, side * half, t))
        both.chip_copy(t).start()

        @pl.when(t == ALONE * X)
        def _():
            alone.after_chip(ALONE * X - 1)

        @pl.when(t == ALONE * X + 4)
        def _():
            alone.after_x(ALONE - 1)
            alone.z_copy(ALONE - 1).start()

        @pl.when(t >= ALONE * X + 2)
        def _():
            both.after_chip(t - 2)

        @pl.when((t % X == 2) & (t >= ALONE * X + 10))
        def _():
            both.after_x(t // X - 2)
            both.z_copy(t // X - 2).start()

        return carry

    lax.fori_loop(ALONE * X, Z * X, step_both, 0)
    both.after_chip(LAST - 1)
    both.after_x(Z - 2)
    both.z_copy(Z - 2).start()
    both.after_chip(LAST)
    own = jnp.zeros((examples, LANES), F32)
    for group in range(ALONE):
        alone.z_copy(group).wait_recv()
        own = own + got_a[group]
    both.after_x(Z - 1)
    pair = rows_b[Z - 1 - ALONE]
    for group in range(ALONE, Z - 1):
        both.z_copy(group).wait_recv()
        pair = pair + got_b[group - ALONE]

    ybuf[y] = pair.reshape(2, examples, LANES)
    ybuf[y, side] = ybuf[y, side] + own

    def y_copy(d):
        return send(ybuf.at[y], ybuf.at[y], ys.at[d - 1], yr.at[d - 1], (me, (y + d) % Y))

    for d in range(1, Y):
        y_copy(d).start()
    for d in range(1, Y):
        y_copy(d).wait_recv()
    for e in range(Y):
        blocks[e] = ybuf[e, e % 2] + ybuf[e + 1 - 2 * (e % 2), e % 2]
    total = blocks[y]
    every = blocks[...].reshape(Y * examples, LANES)

    products = contract(total, every)
    squares = contract(jnp.ones((8, LANES), F32), every * every)
    send1[...] = jnp.zeros_like(send1)
    for j in range(XC):
        send1[j, :, : Y * examples] = products[j * Z : (j + 1) * Z, :]
        for h in range(2):
            send1[j, h : h + 1, Y * examples :] = squares[:1, h * LANES : (h + 1) * LANES]

    def send1_copy(d):
        to = (xc + d) % XC
        return send(send1.at[to], recv1.at[d - 1], s1s.at[d - 1], s1r.at[d - 1], at_xc(to))

    for d in range(1, XC):
        send1_copy(d).start()
    block = send1[xc]
    for d in range(1, XC):
        send1_copy(d).wait_recv()
        block = block + recv1[d - 1]
    planes[z] = block

    def plane_copy(d):
        return send(planes.at[z], planes.at[z], s2s.at[d - 1], s2r.at[d - 1], at(x, (z + d) % Z, c))

    for d in FARTHEST_FIRST:
        plane_copy(d).start()
    for d in range(1, Z):
        plane_copy(d).wait_recv()
    block = planes[0]
    for j in range(1, Z):
        block = block + planes[j]

    root_mean = jnp.sqrt(block[:2, Y * examples :] / features + 1e-06)
    example = y * examples + xc * Z + lax.broadcasted_iota(jnp.int32, (Z, LANES), 0)
    lane = lax.broadcasted_iota(jnp.int32, (Z, LANES), 1)
    labels = lax.broadcasted_iota(jnp.int32, (LANES, LANES), 0)
    own_root = jnp.zeros((Z, 1), F32)
    score, count = jnp.zeros((Z, LANES), F32), jnp.zeros((Z, LANES), F32)
    for h in range(2):
        row = jnp.broadcast_to(root_mean[h : h + 1, :], (Z, LANES))
        own_root = own_root + jnp.sum(jnp.where(lane + h * LANES == example, row, 0.0), axis=1, keepdims=True)
        onehot = (labels == group_ref[h : h + 1, :]).astype(F32)
        score = score + contract(block[:, h * LANES : (h + 1) * LANES] / row, onehot)
        count = count + contract(jnp.ones((Z, LANES), F32), onehot)
    count = jnp.where(count == 0, 1.0, count)
    scored[xc] = score / own_root / (count * features)

    def score_copy(d):
        return send(scored.at[xc], scored.at[xc], o1s.at[d - 1], o1r.at[d - 1], at_xc((xc + d) % XC))

    for d in range(1, XC):
        score_copy(d).start()

    here = y * examples + lax.broadcasted_iota(jnp.int32, (examples, LANES), 0)
    lane = lax.broadcasted_iota(jnp.int32, (examples, LANES), 1)
    column = jnp.zeros((examples, 1), F32)
    for h in range(2):
        row = jnp.broadcast_to(root_mean[h : h + 1, :], (examples, LANES))
        column = column + jnp.sum(jnp.where(lane + h * LANES == here, row, 0.0), axis=1, keepdims=True)
    f_ref[...] = total / column

    for d in range(1, XC):
        score_copy(d).wait_recv()
    s_ref[...] = scored[...].reshape(examples, LANES)[:, :GROUPS]

    exchange.wait_send()
    alone.sent(ALONE)
    both.sent(Z)
    for d in range(1, Y):
        y_copy(d).wait_send()
    for d in range(1, XC):
        send1_copy(d).wait_send()
        score_copy(d).wait_send()
    for d in range(1, Z):
        plane_copy(d).wait_send()


def solution(mesh):
    def shards(gradients, m_state, v_state, row_seeds, col_seeds, group_of):
        examples, params = gradients.shape
        rows = (-1, LANES)
        dma, vmem = pltpu.SemaphoreType.DMA, pltpu.VMEM
        wide = (Y * examples) + LANES

        def buffers(groups, rows):
            block = (rows, LANES)
            return [
                vmem((groups * X, 2, *block), F32),
                vmem((groups * X, *block), F32),
                vmem((groups, X, *block), F32),
                vmem((groups, X, *block), F32),
                vmem((groups, *block), F32),
                vmem((groups, *block), F32),
            ]

        def semaphores(groups):
            return [
                dma((groups * X,)), dma((groups * X,)),
                dma((groups, X)), dma((groups, X)),
                dma((groups,)), dma((groups,)),
            ]

        arguments = [
            gradients, m_state.reshape(rows), v_state.reshape(rows), row_seeds.reshape(rows),
            col_seeds.reshape(rows), group_of.reshape(rows),
        ]
        return pl.pallas_call(
            kernel,
            out_shape=(
                jax.ShapeDtypeStruct((examples, LANES), F32),
                jax.ShapeDtypeStruct((examples, GROUPS), F32),
            ),
            in_specs=[pl.BlockSpec(memory_space=pltpu.HBM)] * 6,
            out_specs=[pl.BlockSpec(memory_space=pltpu.VMEM)] * 2,
            scratch_shapes=[
                *[vmem(array.shape, array.dtype) for array in arguments],
                dma((6,)),
                vmem((examples, params), jnp.bfloat16),
                vmem((2, examples, params // 2), jnp.bfloat16),
                vmem((examples, params // 2), F32),
                vmem((params, LANES), jnp.int32),
                *buffers(ALONE, examples),
                *buffers(Z - ALONE, 2 * examples),
                vmem((Y, 2, examples, LANES), F32),
                vmem((Y, examples, LANES), F32),
                vmem((XC, Z, wide), F32),
                vmem((XC - 1, Z, wide), F32),
                vmem((Z, Z, wide), F32),
                vmem((XC, Z, LANES), F32),
                dma((1,)), dma((1,)),
                *semaphores(ALONE),
                *semaphores(Z - ALONE),
                dma((Y - 1,)), dma((Y - 1,)),
                dma((XC - 1,)), dma((XC - 1,)),
                dma((Z - 1,)), dma((Z - 1,)),
                dma((XC - 1,)), dma((XC - 1,)),
            ],
            compiler_params=pltpu.CompilerParams(
                collective_id=0, has_side_effects=True, vmem_limit_bytes=63 << 20
            ),
            name="features_and_scores",
        )(*arguments)

    in_specs = (P("ex", "param"), P("param"), P("param"), P("param"), P(), P())
    out_specs = (P("ex", "param"), P("ex", None))
    return jax.shard_map(shards, mesh=mesh, in_specs=in_specs, out_specs=out_specs, check_vma=False)
```

```python
import functools

import jax
import jax.numpy as jnp
from jax import lax
from jax.experimental import pallas as pl
from jax.experimental.pallas import tpu as pltpu
from jax.sharding import PartitionSpec as P

GROUPS = 57
X, Z, C, Y = 4, 8, 2, 4
XC = X * C
LANES = 128
ALONE = 4
LATE = 2
LAST = Z * X - 1
FARTHEST_FIRST = (4, 3, 5, 2, 6, 1, 7)
MESH = pl.DeviceIdType.MESH
HIGH = lax.Precision.HIGHEST
F32 = jnp.float32

FACTOR = (739982445 << 4) & 0xFFFFFFFF
FACTOR = FACTOR - (1 << 32) if FACTOR >= 1 << 31 else FACTOR


def signs_of(product):
    mixed = product ^ (product >> 15)
    mixed = mixed * jnp.int32(FACTOR)
    mixed = mixed ^ (mixed >> 13)
    return jnp.where(mixed.astype(jnp.int16) < jnp.int16(0), jnp.bfloat16(-1), jnp.bfloat16(1))


def update_of(grad, mean, square):
    first = 0.9 * mean + 0.1 * grad
    second = 0.999 * square + 0.001 * grad * grad
    return (first / (jnp.sqrt(second) + 1e-08)).astype(jnp.bfloat16)


def contract(a, b):
    return lax.dot_general(a, b, (((1,), (1,)), ((), ())), precision=HIGH, preferred_element_type=F32)


def remote(src, dst, send_sem, recv_sem, device):
    return pltpu.make_async_remote_copy(
        src_ref=src, dst_ref=dst, send_sem=send_sem, recv_sem=recv_sem,
        device_id=device, device_id_type=MESH,
    )


class Sums:
    def __init__(self, begin, at, x, z, c, buffers, semaphores):
        self.begin, self.at, self.x, self.z, self.c = begin, at, x, z, c
        self.part, self.chip, self.sum, self.cols, self.rows, self.got = buffers
        self.cs, self.cr, self.xs, self.xr, self.zs, self.zr = semaphores

    def slot(self, t):
        return t // X - self.begin, t % X

    def put(self, t, value):
        i = t - self.begin * X
        self.part[i, 0] = value[:, :LANES]
        self.part[i, 1] = value[:, LANES:]

    def chip_copy(self, t):
        i = t - self.begin * X
        return remote(
            self.part.at[i, 1 - self.c], self.chip.at[i], self.cs.at[i], self.cr.at[i],
            self.at(self.x, self.z, 1 - self.c),
        )

    def x_copy(self, t):
        i = self.slot(t)
        to = self.at((self.x + 1 + t % X) % X, self.z, self.c)
        return remote(self.sum.at[i], self.cols.at[i], self.xs.at[i], self.xr.at[i], to)

    def z_copy(self, group):
        i = group - self.begin
        to = self.at(self.x, (self.z + 1 + group) % Z, self.c)
        return remote(self.rows.at[i], self.got.at[i], self.zs.at[i], self.zr.at[i], to)

    def after_chip(self, t):
        i = t - self.begin * X
        self.chip_copy(t).wait_recv()
        self.sum[self.slot(t)] = self.part[i, self.c] + self.chip[i]

        @pl.when(t % X < X - 1)
        def _():
            self.x_copy(t).start()

    def after_x(self, group):
        i = group - self.begin
        for j in range(X - 1):
            self.x_copy(group * X + j).wait_recv()
        self.rows[i] = self.sum[i, X - 1] + self.cols[i, 0] + self.cols[i, 1] + self.cols[i, 2]

    def sent(self, end):
        def one(t, carry):
            self.chip_copy(t).wait_send()

            @pl.when(t % X < X - 1)
            def _():
                self.x_copy(t).wait_send()

            return carry

        lax.fori_loop(self.begin * X, end * X, one, 0)
        for group in range(self.begin, min(end, Z - 1)):
            self.z_copy(group).wait_send()


def kernel(
    g_in, m_in, v_in, r_in, k_in, group_in,
    f_ref, s_ref,
    g_ref, m_ref, v_ref, r_ref, k_ref, group_ref, in_sems,
    u_own, u_both, g_other, seeds,
    part_a, chip_a, sum_a, cols_a, rows_a, got_a,
    part_b, chip_b, sum_b, cols_b, rows_b, got_b,
    ybuf, blocks, send1, recv1, planes, scored,
    gs, gr,
    cs_a, cr_a, xs_a, xr_a, zs_a, zr_a,
    cs_b, cr_b, xs_b, xr_b, zs_b, zr_b,
    ys, yr, s1s, s1r, s2s, s2r, o1s, o1r,
):
    me, y = lax.axis_index("param"), lax.axis_index("ex")
    x, z, c = me // (Z * C), (me // C) % Z, me % C
    xc = x * C + c
    side = y % 2
    partner = (me, y + 1 - 2 * side)
    examples, params = g_ref.shape
    half = params // 2
    features = k_ref.shape[0] * LANES
    send = remote

    inputs = [
        pltpu.make_async_copy(src, dst, in_sems.at[i])
        for i, (src, dst) in enumerate(
            [(g_in, g_ref), (m_in, m_ref), (v_in, v_ref), (r_in, r_ref), (k_in, k_ref), (group_in, group_ref)]
        )
    ]
    for copy in inputs:
        copy.start()

    def at(x_to, z_to, c_to):
        return ((x_to * Z + z_to) * C + c_to, y)

    def at_xc(to):
        return at(to // C, z, to % C)

    barrier = pltpu.get_barrier_semaphore()

    def greet(device):
        pl.semaphore_signal(barrier, inc=1, device_id=device, device_id_type=MESH)

    for d in FARTHEST_FIRST:
        greet(at(x, (z + d) % Z, c))
    for d in range(1, XC):
        greet(at_xc((xc + d) % XC))
    for d in range(1, Y):
        greet((me, (y + d) % Y))
    for copy in inputs:
        copy.wait()

    def prepare(i, carry):
        for k in range(4):
            row = i * 4 + k
            lanes = pl.ds(pl.multiple_of(row * LANES, LANES), LANES)
            u_own[:, lanes] = update_of(g_ref[:, lanes], m_ref[pl.ds(row, 1), :], v_ref[pl.ds(row, 1), :])
            seeds[lanes, :] = jnp.broadcast_to(r_ref[pl.ds(row, 1), :], (LANES, LANES)).T
        return carry

    lax.fori_loop(0, params // LANES // 4, prepare, 0)

    def chunk(update, depth, base, t):
        x_to, z_to = (x + 1 + t % X) % X, (z + 1 + t // X) % Z
        row = (x_to * Z + z_to) * C
        left, right = k_ref[pl.ds(row, 1), :], k_ref[pl.ds(row + 1, 1), :]
        strips = []
        for p in range(0, depth, 16):
            seed = seeds[pl.ds(pl.multiple_of(base + p, 16), 16), :]
            strips.append(jnp.concatenate([signs_of(seed * left), signs_of(seed * right)], axis=1))
        return jnp.dot(update, jnp.concatenate(strips, axis=0), preferred_element_type=F32)

    alone = Sums(
        0, at, x, z, c,
        (part_a, chip_a, sum_a, cols_a, rows_a, got_a), (cs_a, cr_a, xs_a, xr_a, zs_a, zr_a),
    )
    both = Sums(
        ALONE, at, x, z, c,
        (part_b, chip_b, sum_b, cols_b, rows_b, got_b), (cs_b, cr_b, xs_b, xr_b, zs_b, zr_b),
    )
    exchange = send(
        g_ref.at[:, pl.ds(pl.multiple_of((1 - side) * half, half), half)], g_other, gs.at[0], gr.at[0], partner
    )

    def pair_alone(i, carry):
        t = 2 * i
        alone.put(t, chunk(u_own[...], params, 0, t))
        alone.put(t + 1, chunk(u_own[...], params, 0, t + 1))

        @pl.when(t == LATE)
        def _():
            pl.semaphore_wait(barrier, (XC - 1) + (Z - 1) + (Y - 1))
            exchange.start()
            for early in range(LATE):
                alone.chip_copy(early).start()

        @pl.when(t >= LATE)
        def _():
            alone.chip_copy(t).start()
            alone.chip_copy(t + 1).start()

        @pl.when(t == LATE + 2)
        def _():
            for early in range(LATE):
                alone.after_chip(early)

        @pl.when(t >= LATE + 2)
        def _():
            alone.after_chip(t - 2)
            alone.after_chip(t - 1)

        @pl.when((t % X == 0) & (t >= LATE + 6))
        def _():
            alone.after_x(t // X - 2)
            alone.z_copy(t // X - 2).start()

        return carry

    lax.fori_loop(0, ALONE * X // 2, pair_alone, 0)

    u_both[side] = u_own[:, pl.ds(pl.multiple_of(side * half, half), half)]
    exchange.wait_recv()

    def prepare_other(i, carry):
        for k in range(4):
            lanes = pl.ds(pl.multiple_of((i * 4 + k) * LANES, LANES), LANES)
            row = side * (half // LANES) + i * 4 + k
            u_both[1 - side, :, lanes] = update_of(g_other[:, lanes], m_ref[pl.ds(row, 1), :], v_ref[pl.ds(row, 1), :])
        return carry

    lax.fori_loop(0, half // LANES // 4, prepare_other, 0)

    def chunk_both(t):
        both.put(t, chunk(u_both[...].reshape(2 * examples, half), half, side * half, t))

    def pair_both(i, carry):
        t = ALONE * X + 2 * i
        chunk_both(t)
        chunk_both(t + 1)
        both.chip_copy(t).start()
        both.chip_copy(t + 1).start()

        @pl.when(i == 0)
        def _():
            alone.after_chip(ALONE * X - 2)
            alone.after_chip(ALONE * X - 1)
            alone.after_x(ALONE - 2)
            alone.z_copy(ALONE - 2).start()

        @pl.when(i == 3)
        def _():
            alone.after_x(ALONE - 1)
            alone.z_copy(ALONE - 1).start()

        @pl.when(i >= 1)
        def _():
            both.after_chip(t - 2)
            both.after_chip(t - 1)

        @pl.when((i % 2 == 1) & (i >= 5))
        def _():
            group = ALONE + (i - 5) // 2
            both.after_x(group)
            both.z_copy(group).start()

        return carry

    def step_both(t, carry):
        chunk_both(t)
        both.chip_copy(t).start()
        both.after_chip(t - 2)

        @pl.when(t == LAST - 1)
        def _():
            both.after_x(Z - 3)
            both.z_copy(Z - 3).start()

        return carry

    lax.fori_loop(0, (Z - 1 - ALONE) * X // 2, pair_both, 0)
    lax.fori_loop((Z - 1) * X, Z * X, step_both, 0)
    both.after_chip(LAST - 1)
    both.after_x(Z - 2)
    both.z_copy(Z - 2).start()
    both.after_chip(LAST)
    own = jnp.zeros((examples, LANES), F32)
    for group in range(ALONE):
        alone.z_copy(group).wait_recv()
        own = own + got_a[group]
    both.after_x(Z - 1)
    pair = rows_b[Z - 1 - ALONE]
    for group in range(ALONE, Z - 1):
        both.z_copy(group).wait_recv()
        pair = pair + got_b[group - ALONE]

    ybuf[y] = pair.reshape(2, examples, LANES)
    ybuf[y, side] = ybuf[y, side] + own

    def y_copy(d):
        return send(ybuf.at[y], ybuf.at[y], ys.at[d - 1], yr.at[d - 1], (me, (y + d) % Y))

    for d in range(1, Y):
        y_copy(d).start()
    exchange.wait_send()
    alone.sent(ALONE)
    both.sent(Z)
    for d in range(1, Y):
        y_copy(d).wait_recv()
    for e in range(Y):
        blocks[e] = ybuf[e, e % 2] + ybuf[e + 1 - 2 * (e % 2), e % 2]
    total = blocks[y]
    every = blocks[...].reshape(Y * examples, LANES)

    products = contract(total, every)
    squares = contract(jnp.ones((8, LANES), F32), every * every)
    send1[...] = jnp.zeros_like(send1)
    for j in range(XC):
        send1[j, :, : Y * examples] = products[j * Z : (j + 1) * Z, :]
        for h in range(2):
            send1[j, h : h + 1, Y * examples :] = squares[:1, h * LANES : (h + 1) * LANES]

    def send1_copy(d):
        to = (xc + d) % XC
        return send(send1.at[to], recv1.at[d - 1], s1s.at[d - 1], s1r.at[d - 1], at_xc(to))

    for d in range(1, XC):
        send1_copy(d).start()
    for d in range(1, Y):
        y_copy(d).wait_send()
    block = send1[xc]
    for d in range(1, XC):
        send1_copy(d).wait_recv()
        block = block + recv1[d - 1]
    planes[z] = block

    def plane_copy(d):
        return send(planes.at[z], planes.at[z], s2s.at[d - 1], s2r.at[d - 1], at(x, (z + d) % Z, c))

    for d in FARTHEST_FIRST:
        plane_copy(d).start()
    for d in range(1, XC):
        send1_copy(d).wait_send()
    for d in range(1, Z):
        plane_copy(d).wait_recv()
    block = planes[0]
    for j in range(1, Z):
        block = block + planes[j]

    root_mean = jnp.sqrt(block[:2, Y * examples :] / features + 1e-06)
    example = y * examples + xc * Z + lax.broadcasted_iota(jnp.int32, (Z, LANES), 0)
    lane = lax.broadcasted_iota(jnp.int32, (Z, LANES), 1)
    labels = lax.broadcasted_iota(jnp.int32, (LANES, LANES), 0)
    own_root = jnp.zeros((Z, 1), F32)
    score, count = jnp.zeros((Z, LANES), F32), jnp.zeros((Z, LANES), F32)
    for h in range(2):
        row = jnp.broadcast_to(root_mean[h : h + 1, :], (Z, LANES))
        own_root = own_root + jnp.sum(jnp.where(lane + h * LANES == example, row, 0.0), axis=1, keepdims=True)
        onehot = (labels == group_ref[h : h + 1, :]).astype(F32)
        score = score + contract(block[:, h * LANES : (h + 1) * LANES] / row, onehot)
        count = count + contract(jnp.ones((Z, LANES), F32), onehot)
    count = jnp.where(count == 0, 1.0, count)
    scored[xc] = score / own_root / (count * features)

    def score_copy(d):
        return send(scored.at[xc], scored.at[xc], o1s.at[d - 1], o1r.at[d - 1], at_xc((xc + d) % XC))

    for d in range(1, XC):
        score_copy(d).start()
    for d in range(1, Z):
        plane_copy(d).wait_send()

    here = y * examples + lax.broadcasted_iota(jnp.int32, (examples, LANES), 0)
    lane = lax.broadcasted_iota(jnp.int32, (examples, LANES), 1)
    column = jnp.zeros((examples, 1), F32)
    for h in range(2):
        row = jnp.broadcast_to(root_mean[h : h + 1, :], (examples, LANES))
        column = column + jnp.sum(jnp.where(lane + h * LANES == here, row, 0.0), axis=1, keepdims=True)
    f_ref[...] = total / column

    for d in range(1, XC):
        score_copy(d).wait_recv()
    s_ref[...] = scored[...].reshape(examples, LANES)[:, :GROUPS]

    for d in range(1, XC):
        score_copy(d).wait_send()


def solution(mesh):
    def shards(gradients, m_state, v_state, row_seeds, col_seeds, group_of):
        examples, params = gradients.shape
        rows = (-1, LANES)
        dma, vmem = pltpu.SemaphoreType.DMA, pltpu.VMEM
        wide = (Y * examples) + LANES

        def buffers(groups, rows):
            block = (rows, LANES)
            return [
                vmem((groups * X, 2, *block), F32),
                vmem((groups * X, *block), F32),
                vmem((groups, X, *block), F32),
                vmem((groups, X, *block), F32),
                vmem((groups, *block), F32),
                vmem((groups, *block), F32),
            ]

        def semaphores(groups):
            return [
                dma((groups * X,)), dma((groups * X,)),
                dma((groups, X)), dma((groups, X)),
                dma((groups,)), dma((groups,)),
            ]

        arguments = [
            gradients, m_state.reshape(rows), v_state.reshape(rows), row_seeds.reshape(rows),
            col_seeds.reshape(rows), group_of.reshape(rows),
        ]
        return pl.pallas_call(
            kernel,
            out_shape=(
                jax.ShapeDtypeStruct((examples, LANES), F32),
                jax.ShapeDtypeStruct((examples, GROUPS), F32),
            ),
            in_specs=[pl.BlockSpec(memory_space=pltpu.HBM)] * 6,
            out_specs=[pl.BlockSpec(memory_space=pltpu.VMEM)] * 2,
            scratch_shapes=[
                *[vmem(array.shape, array.dtype) for array in arguments],
                dma((6,)),
                vmem((examples, params), jnp.bfloat16),
                vmem((2, examples, params // 2), jnp.bfloat16),
                vmem((examples, params // 2), F32),
                vmem((params, LANES), jnp.int32),
                *buffers(ALONE, examples),
                *buffers(Z - ALONE, 2 * examples),
                vmem((Y, 2, examples, LANES), F32),
                vmem((Y, examples, LANES), F32),
                vmem((XC, Z, wide), F32),
                vmem((XC - 1, Z, wide), F32),
                vmem((Z, Z, wide), F32),
                vmem((XC, Z, LANES), F32),
                dma((1,)), dma((1,)),
                *semaphores(ALONE),
                *semaphores(Z - ALONE),
                dma((Y - 1,)), dma((Y - 1,)),
                dma((XC - 1,)), dma((XC - 1,)),
                dma((Z - 1,)), dma((Z - 1,)),
                dma((XC - 1,)), dma((XC - 1,)),
            ],
            compiler_params=pltpu.CompilerParams(
                collective_id=0, has_side_effects=True, vmem_limit_bytes=48 << 20
            ),
            name="features_and_scores",
        )(*[pltpu.with_memory_space_constraint(array, pltpu.HBM) for array in arguments])

    in_specs = (P("ex", "param"), P("param"), P("param"), P("param"), P(), P())
    out_specs = (P("ex", "param"), P("ex", None))
    return jax.shard_map(shards, mesh=mesh, in_specs=in_specs, out_specs=out_specs, check_vma=False)
```

```python
import functools

import jax
import jax.numpy as jnp
from jax import lax
from jax.experimental import pallas as pl
from jax.experimental.pallas import tpu as pltpu
from jax.sharding import PartitionSpec as P

GROUPS = 57
X, Z, C, Y = 4, 8, 2, 4
XC = X * C
LANES = 128
ALONE = 4
LAST = Z * X - 1
FARTHEST_FIRST = (4, 3, 5, 2, 6, 1, 7)
MESH = pl.DeviceIdType.MESH
HIGH = lax.Precision.HIGHEST
F32 = jnp.float32

FACTOR = (739982445 << 4) & 0xFFFFFFFF
FACTOR = FACTOR - (1 << 32) if FACTOR >= 1 << 31 else FACTOR


def signs_of(product):
    mixed = product ^ (product >> 15)
    mixed = mixed * jnp.int32(FACTOR)
    mixed = mixed ^ (mixed >> 13)
    return jnp.where(mixed.astype(jnp.int16) < jnp.int16(0), jnp.bfloat16(-1), jnp.bfloat16(1))


def update_of(grad, mean, square):
    first = 0.9 * mean + 0.1 * grad
    second = 0.999 * square + 0.001 * grad * grad
    return (first / (jnp.sqrt(second) + 1e-08)).astype(jnp.bfloat16)


def contract(a, b):
    return lax.dot_general(a, b, (((1,), (1,)), ((), ())), precision=HIGH, preferred_element_type=F32)


def remote(src, dst, send_sem, recv_sem, device):
    return pltpu.make_async_remote_copy(
        src_ref=src, dst_ref=dst, send_sem=send_sem, recv_sem=recv_sem,
        device_id=device, device_id_type=MESH,
    )


class Sums:
    def __init__(self, begin, at, x, z, c, buffers, semaphores):
        self.begin, self.at, self.x, self.z, self.c = begin, at, x, z, c
        self.part, self.chip, self.sum, self.cols, self.rows, self.got = buffers
        self.cs, self.cr, self.xs, self.xr, self.zs, self.zr = semaphores

    def slot(self, t):
        return t // X - self.begin, t % X

    def put(self, t, value):
        i = t - self.begin * X
        self.part[i, 0] = value[:, :LANES]
        self.part[i, 1] = value[:, LANES:]

    def chip_copy(self, t):
        i = t - self.begin * X
        return remote(
            self.part.at[i, 1 - self.c], self.chip.at[i], self.cs.at[i], self.cr.at[i],
            self.at(self.x, self.z, 1 - self.c),
        )

    def x_copy(self, t):
        i = self.slot(t)
        to = self.at((self.x + 1 + t % X) % X, self.z, self.c)
        return remote(self.sum.at[i], self.cols.at[i], self.xs.at[i], self.xr.at[i], to)

    def z_copy(self, group):
        i = group - self.begin
        to = self.at(self.x, (self.z + 1 + group) % Z, self.c)
        return remote(self.rows.at[i], self.got.at[i], self.zs.at[i], self.zr.at[i], to)

    def after_chip(self, t):
        i = t - self.begin * X
        self.chip_copy(t).wait_recv()
        self.sum[self.slot(t)] = self.part[i, self.c] + self.chip[i]

        @pl.when(t % X < X - 1)
        def _():
            self.x_copy(t).start()

    def after_x(self, group):
        i = group - self.begin
        for j in range(X - 1):
            self.x_copy(group * X + j).wait_recv()
        self.rows[i] = self.sum[i, X - 1] + self.cols[i, 0] + self.cols[i, 1] + self.cols[i, 2]

    def sent(self, end):
        def one(t, carry):
            self.chip_copy(t).wait_send()

            @pl.when(t % X < X - 1)
            def _():
                self.x_copy(t).wait_send()

            return carry

        lax.fori_loop(self.begin * X, end * X, one, 0)
        for group in range(self.begin, min(end, Z - 1)):
            self.z_copy(group).wait_send()


def kernel(
    g_in, m_in, v_in, r_in, k_in, group_in,
    f_ref, s_ref,
    g_ref, m_ref, v_ref, r_ref, k_ref, group_ref, in_sems,
    u_own, u_both, g_other, seeds,
    part_a, chip_a, sum_a, cols_a, rows_a, got_a,
    part_b, chip_b, sum_b, cols_b, rows_b, got_b,
    ybuf, blocks, send1, recv1, planes, scored,
    gs, gr,
    cs_a, cr_a, xs_a, xr_a, zs_a, zr_a,
    cs_b, cr_b, xs_b, xr_b, zs_b, zr_b,
    ys, yr, s1s, s1r, s2s, s2r, o1s, o1r,
):
    me, y = lax.axis_index("param"), lax.axis_index("ex")
    x, z, c = me // (Z * C), (me // C) % Z, me % C
    xc = x * C + c
    side = y % 2
    partner = (me, y + 1 - 2 * side)
    examples, params = g_ref.shape
    half = params // 2
    features = k_ref.shape[0] * LANES
    send = remote

    inputs = [
        pltpu.make_async_copy(src, dst, in_sems.at[i])
        for i, (src, dst) in enumerate(
            [(g_in, g_ref), (m_in, m_ref), (v_in, v_ref), (r_in, r_ref), (k_in, k_ref), (group_in, group_ref)]
        )
    ]
    for copy in inputs:
        copy.start()

    def at(x_to, z_to, c_to):
        return ((x_to * Z + z_to) * C + c_to, y)

    def at_xc(to):
        return at(to // C, z, to % C)

    barrier = pltpu.get_barrier_semaphore()

    def greet(device):
        pl.semaphore_signal(barrier, inc=1, device_id=device, device_id_type=MESH)

    for d in FARTHEST_FIRST:
        greet(at(x, (z + d) % Z, c))
    for d in range(1, XC):
        greet(at_xc((xc + d) % XC))
    for d in range(1, Y):
        greet((me, (y + d) % Y))
    for copy in inputs:
        copy.wait()

    def prepare(i, carry):
        for k in range(4):
            row = i * 4 + k
            lanes = pl.ds(pl.multiple_of(row * LANES, LANES), LANES)
            u_own[:, lanes] = update_of(g_ref[:, lanes], m_ref[pl.ds(row, 1), :], v_ref[pl.ds(row, 1), :])
            seeds[lanes, :] = jnp.broadcast_to(r_ref[pl.ds(row, 1), :], (LANES, LANES)).T
        return carry

    lax.fori_loop(0, params // LANES // 4, prepare, 0)

    def chunk(update, depth, base, t):
        x_to, z_to = (x + 1 + t % X) % X, (z + 1 + t // X) % Z
        row = (x_to * Z + z_to) * C
        left, right = k_ref[pl.ds(row, 1), :], k_ref[pl.ds(row + 1, 1), :]
        strips = []
        for p in range(0, depth, 16):
            seed = seeds[pl.ds(pl.multiple_of(base + p, 16), 16), :]
            strips.append(jnp.concatenate([signs_of(seed * left), signs_of(seed * right)], axis=1))
        return jnp.dot(update, jnp.concatenate(strips, axis=0), preferred_element_type=F32)

    alone = Sums(
        0, at, x, z, c,
        (part_a, chip_a, sum_a, cols_a, rows_a, got_a), (cs_a, cr_a, xs_a, xr_a, zs_a, zr_a),
    )
    both = Sums(
        ALONE, at, x, z, c,
        (part_b, chip_b, sum_b, cols_b, rows_b, got_b), (cs_b, cr_b, xs_b, xr_b, zs_b, zr_b),
    )
    exchange = send(
        g_ref.at[:, pl.ds(pl.multiple_of((1 - side) * half, half), half)], g_other, gs.at[0], gr.at[0], partner
    )

    def pair_alone(i, carry):
        t = 2 * i
        alone.put(t, chunk(u_own[...], params, 0, t))
        alone.put(t + 1, chunk(u_own[...], params, 0, t + 1))

        @pl.when(i == 0)
        def _():
            pl.semaphore_wait(barrier, (XC - 1) + (Z - 1) + (Y - 1))
            exchange.start()

        alone.chip_copy(t).start()
        alone.chip_copy(t + 1).start()

        @pl.when(i >= 1)
        def _():
            alone.after_chip(t - 2)
            alone.after_chip(t - 1)

        @pl.when((t % X == 0) & (t >= 2 * X))
        def _():
            alone.after_x(t // X - 2)
            alone.z_copy(t // X - 2).start()

        return carry

    lax.fori_loop(0, ALONE * X // 2, pair_alone, 0)

    u_both[side] = u_own[:, pl.ds(pl.multiple_of(side * half, half), half)]
    exchange.wait_recv()

    def prepare_other(i, carry):
        for k in range(4):
            lanes = pl.ds(pl.multiple_of((i * 4 + k) * LANES, LANES), LANES)
            row = side * (half // LANES) + i * 4 + k
            u_both[1 - side, :, lanes] = update_of(g_other[:, lanes], m_ref[pl.ds(row, 1), :], v_ref[pl.ds(row, 1), :])
        return carry

    lax.fori_loop(0, half // LANES // 4, prepare_other, 0)

    def chunk_both(t):
        both.put(t, chunk(u_both[...].reshape(2 * examples, half), half, side * half, t))

    def pair_both(i, carry):
        t = ALONE * X + 2 * i
        chunk_both(t)
        chunk_both(t + 1)
        both.chip_copy(t).start()
        both.chip_copy(t + 1).start()

        @pl.when(i == 0)
        def _():
            alone.after_chip(ALONE * X - 2)
            alone.after_chip(ALONE * X - 1)
            alone.after_x(ALONE - 2)
            alone.z_copy(ALONE - 2).start()

        @pl.when(i == 3)
        def _():
            alone.after_x(ALONE - 1)
            alone.z_copy(ALONE - 1).start()

        @pl.when(i >= 1)
        def _():
            both.after_chip(t - 2)
            both.after_chip(t - 1)

        @pl.when((i % 2 == 1) & (i >= 5))
        def _():
            group = ALONE + (i - 5) // 2
            both.after_x(group)
            both.z_copy(group).start()

        return carry

    def step_both(t, carry):
        chunk_both(t)
        both.chip_copy(t).start()
        both.after_chip(t - 2)

        @pl.when(t == LAST - 1)
        def _():
            both.after_x(Z - 3)
            both.z_copy(Z - 3).start()

        return carry

    lax.fori_loop(0, (Z - 1 - ALONE) * X // 2, pair_both, 0)
    lax.fori_loop((Z - 1) * X, Z * X, step_both, 0)
    both.after_chip(LAST - 1)
    both.after_x(Z - 2)
    both.z_copy(Z - 2).start()
    both.after_chip(LAST)
    own = jnp.zeros((examples, LANES), F32)
    for group in range(ALONE):
        alone.z_copy(group).wait_recv()
        own = own + got_a[group]
    both.after_x(Z - 1)
    pair = rows_b[Z - 1 - ALONE]
    for group in range(ALONE, Z - 1):
        both.z_copy(group).wait_recv()
        pair = pair + got_b[group - ALONE]

    ybuf[y] = pair.reshape(2, examples, LANES)
    ybuf[y, side] = ybuf[y, side] + own

    def y_copy(d):
        return send(ybuf.at[y], ybuf.at[y], ys.at[d - 1], yr.at[d - 1], (me, (y + d) % Y))

    for d in range(1, Y):
        y_copy(d).start()
    exchange.wait_send()
    alone.sent(ALONE)
    both.sent(Z)
    for d in range(1, Y):
        y_copy(d).wait_recv()
    for e in range(Y):
        blocks[e] = ybuf[e, e % 2] + ybuf[e + 1 - 2 * (e % 2), e % 2]
    total = blocks[y]
    every = blocks[...].reshape(Y * examples, LANES)

    products = contract(total, every)
    squares = contract(jnp.ones((8, LANES), F32), every * every)
    send1[...] = jnp.zeros_like(send1)
    for j in range(XC):
        send1[j, :, : Y * examples] = products[j * Z : (j + 1) * Z, :]
        for h in range(2):
            send1[j, h : h + 1, Y * examples :] = squares[:1, h * LANES : (h + 1) * LANES]

    def send1_copy(d):
        to = (xc + d) % XC
        return send(send1.at[to], recv1.at[d - 1], s1s.at[d - 1], s1r.at[d - 1], at_xc(to))

    for d in range(1, XC):
        send1_copy(d).start()
    for d in range(1, Y):
        y_copy(d).wait_send()
    block = send1[xc]
    for d in range(1, XC):
        send1_copy(d).wait_recv()
        block = block + recv1[d - 1]
    planes[z] = block

    def plane_copy(d):
        return send(planes.at[z], planes.at[z], s2s.at[d - 1], s2r.at[d - 1], at(x, (z + d) % Z, c))

    for d in FARTHEST_FIRST:
        plane_copy(d).start()
    for d in range(1, XC):
        send1_copy(d).wait_send()
    for d in range(1, Z):
        plane_copy(d).wait_recv()
    block = planes[0]
    for j in range(1, Z):
        block = block + planes[j]

    root_mean = jnp.sqrt(block[:2, Y * examples :] / features + 1e-06)
    example = y * examples + xc * Z + lax.broadcasted_iota(jnp.int32, (Z, LANES), 0)
    lane = lax.broadcasted_iota(jnp.int32, (Z, LANES), 1)
    labels = lax.broadcasted_iota(jnp.int32, (LANES, LANES), 0)
    own_root = jnp.zeros((Z, 1), F32)
    score, count = jnp.zeros((Z, LANES), F32), jnp.zeros((Z, LANES), F32)
    for h in range(2):
        row = jnp.broadcast_to(root_mean[h : h + 1, :], (Z, LANES))
        own_root = own_root + jnp.sum(jnp.where(lane + h * LANES == example, row, 0.0), axis=1, keepdims=True)
        onehot = (labels == group_ref[h : h + 1, :]).astype(F32)
        score = score + contract(block[:, h * LANES : (h + 1) * LANES] / row, onehot)
        count = count + contract(jnp.ones((Z, LANES), F32), onehot)
    count = jnp.where(count == 0, 1.0, count)
    scored[xc] = score / own_root / (count * features)

    def score_copy(d):
        return send(scored.at[xc], scored.at[xc], o1s.at[d - 1], o1r.at[d - 1], at_xc((xc + d) % XC))

    for d in range(1, XC):
        score_copy(d).start()
    for d in range(1, Z):
        plane_copy(d).wait_send()

    here = y * examples + lax.broadcasted_iota(jnp.int32, (examples, LANES), 0)
    lane = lax.broadcasted_iota(jnp.int32, (examples, LANES), 1)
    column = jnp.zeros((examples, 1), F32)
    for h in range(2):
        row = jnp.broadcast_to(root_mean[h : h + 1, :], (examples, LANES))
        column = column + jnp.sum(jnp.where(lane + h * LANES == here, row, 0.0), axis=1, keepdims=True)
    f_ref[...] = total / column

    for d in range(1, XC):
        score_copy(d).wait_recv()
    s_ref[...] = scored[...].reshape(examples, LANES)[:, :GROUPS]

    for d in range(1, XC):
        score_copy(d).wait_send()


def solution(mesh):
    def shards(gradients, m_state, v_state, row_seeds, col_seeds, group_of):
        examples, params = gradients.shape
        rows = (-1, LANES)
        dma, vmem = pltpu.SemaphoreType.DMA, pltpu.VMEM
        wide = (Y * examples) + LANES

        def buffers(groups, rows):
            block = (rows, LANES)
            return [
                vmem((groups * X, 2, *block), F32),
                vmem((groups * X, *block), F32),
                vmem((groups, X, *block), F32),
                vmem((groups, X, *block), F32),
                vmem((groups, *block), F32),
                vmem((groups, *block), F32),
            ]

        def semaphores(groups):
            return [
                dma((groups * X,)), dma((groups * X,)),
                dma((groups, X)), dma((groups, X)),
                dma((groups,)), dma((groups,)),
            ]

        arguments = [
            gradients, m_state.reshape(rows), v_state.reshape(rows), row_seeds.reshape(rows),
            col_seeds.reshape(rows), group_of.reshape(rows),
        ]
        return pl.pallas_call(
            kernel,
            out_shape=(
                jax.ShapeDtypeStruct((examples, LANES), F32),
                jax.ShapeDtypeStruct((examples, GROUPS), F32),
            ),
            in_specs=[pl.BlockSpec(memory_space=pltpu.HBM)] * 6,
            out_specs=[pl.BlockSpec(memory_space=pltpu.VMEM)] * 2,
            scratch_shapes=[
                *[vmem(array.shape, array.dtype) for array in arguments],
                dma((6,)),
                vmem((examples, params), jnp.bfloat16),
                vmem((2, examples, params // 2), jnp.bfloat16),
                vmem((examples, params // 2), F32),
                vmem((params, LANES), jnp.int32),
                *buffers(ALONE, examples),
                *buffers(Z - ALONE, 2 * examples),
                vmem((Y, 2, examples, LANES), F32),
                vmem((Y, examples, LANES), F32),
                vmem((XC, Z, wide), F32),
                vmem((XC - 1, Z, wide), F32),
                vmem((Z, Z, wide), F32),
                vmem((XC, Z, LANES), F32),
                dma((1,)), dma((1,)),
                *semaphores(ALONE),
                *semaphores(Z - ALONE),
                dma((Y - 1,)), dma((Y - 1,)),
                dma((XC - 1,)), dma((XC - 1,)),
                dma((Z - 1,)), dma((Z - 1,)),
                dma((XC - 1,)), dma((XC - 1,)),
            ],
            compiler_params=pltpu.CompilerParams(
                collective_id=0, has_side_effects=True, vmem_limit_bytes=48 << 20
            ),
            name="features_and_scores",
        )(*[pltpu.with_memory_space_constraint(array, pltpu.HBM) for array in arguments])

    in_specs = (P("ex", "param"), P("param"), P("param"), P("param"), P(), P())
    out_specs = (P("ex", "param"), P("ex", None))
    return jax.shard_map(shards, mesh=mesh, in_specs=in_specs, out_specs=out_specs, check_vma=False)
```

```python
import functools

import jax
import jax.numpy as jnp
from jax import lax
from jax.experimental import pallas as pl
from jax.experimental.pallas import tpu as pltpu
from jax.sharding import PartitionSpec as P

GROUPS = 57
X, Z, C, Y = 4, 8, 2, 4
XC = X * C
LANES = 128
ALONE = 4
LAST = Z * X - 1
FARTHEST_FIRST = (4, 3, 5, 2, 6, 1, 7)
MESH = pl.DeviceIdType.MESH
HIGH = lax.Precision.HIGHEST
F32 = jnp.float32

FACTOR = (739982445 << 4) & 0xFFFFFFFF
FACTOR = FACTOR - (1 << 32) if FACTOR >= 1 << 31 else FACTOR


def signs_of(product):
    mixed = product ^ (product >> 15)
    mixed = mixed * jnp.int32(FACTOR)
    mixed = mixed ^ (mixed >> 13)
    return jnp.where(mixed.astype(jnp.int16) < jnp.int16(0), jnp.bfloat16(-1), jnp.bfloat16(1))


def update_of(grad, mean, square):
    first = 0.9 * mean + 0.1 * grad
    second = 0.999 * square + 0.001 * grad * grad
    return (first / (jnp.sqrt(second) + 1e-08)).astype(jnp.bfloat16)


def contract(a, b):
    return lax.dot_general(a, b, (((1,), (1,)), ((), ())), precision=HIGH, preferred_element_type=F32)


def remote(src, dst, send_sem, recv_sem, device):
    return pltpu.make_async_remote_copy(
        src_ref=src, dst_ref=dst, send_sem=send_sem, recv_sem=recv_sem,
        device_id=device, device_id_type=MESH,
    )


class Sums:
    def __init__(self, begin, at, x, z, c, buffers, semaphores):
        self.begin, self.at, self.x, self.z, self.c = begin, at, x, z, c
        self.part, self.chip, self.sum, self.cols, self.rows, self.got = buffers
        self.cs, self.cr, self.xs, self.xr, self.zs, self.zr = semaphores

    def slot(self, t):
        return t // X - self.begin, t % X

    def put(self, t, value):
        i = t - self.begin * X
        self.part[i, 0] = value[:, :LANES]
        self.part[i, 1] = value[:, LANES:]

    def chip_copy(self, t):
        i = t - self.begin * X
        return remote(
            self.part.at[i, 1 - self.c], self.chip.at[i], self.cs.at[i], self.cr.at[i],
            self.at(self.x, self.z, 1 - self.c),
        )

    def x_copy(self, t):
        i = self.slot(t)
        to = self.at((self.x + 1 + t % X) % X, self.z, self.c)
        return remote(self.sum.at[i], self.cols.at[i], self.xs.at[i], self.xr.at[i], to)

    def z_copy(self, group):
        i = group - self.begin
        to = self.at(self.x, (self.z + 1 + group) % Z, self.c)
        return remote(self.rows.at[i], self.got.at[i], self.zs.at[i], self.zr.at[i], to)

    def after_chip(self, t):
        i = t - self.begin * X
        self.chip_copy(t).wait_recv()
        self.sum[self.slot(t)] = self.part[i, self.c] + self.chip[i]

        @pl.when(t % X < X - 1)
        def _():
            self.x_copy(t).start()

    def after_x(self, group):
        i = group - self.begin
        for j in range(X - 1):
            self.x_copy(group * X + j).wait_recv()
        self.rows[i] = self.sum[i, X - 1] + self.cols[i, 0] + self.cols[i, 1] + self.cols[i, 2]

    def sent(self, end):
        def one(t, carry):
            self.chip_copy(t).wait_send()

            @pl.when(t % X < X - 1)
            def _():
                self.x_copy(t).wait_send()

            return carry

        lax.fori_loop(self.begin * X, end * X, one, 0)
        for group in range(self.begin, min(end, Z - 1)):
            self.z_copy(group).wait_send()


def kernel(
    g_in, m_in, v_in, r_in, k_in, group_in,
    f_ref, s_ref,
    g_ref, m_ref, v_ref, r_ref, k_ref, group_ref, in_sems,
    u_own, u_both, g_other, seeds,
    part_a, chip_a, sum_a, cols_a, rows_a, got_a,
    part_b, chip_b, sum_b, cols_b, rows_b, got_b,
    ybuf, blocks, send1, recv1, planes, norm1, norm_recv, norm_planes, scored,
    gs, gr,
    cs_a, cr_a, xs_a, xr_a, zs_a, zr_a,
    cs_b, cr_b, xs_b, xr_b, zs_b, zr_b,
    ys, yr, s1s, s1r, s2s, s2r, n1s, n1r, n2s, n2r, o1s, o1r,
):
    me, y = lax.axis_index("param"), lax.axis_index("ex")
    x, z, c = me // (Z * C), (me // C) % Z, me % C
    xc = x * C + c
    side = y % 2
    partner = (me, y + 1 - 2 * side)
    examples, params = g_ref.shape
    half = params // 2
    features = k_ref.shape[0] * LANES
    send = remote

    inputs = [
        pltpu.make_async_copy(src, dst, in_sems.at[i])
        for i, (src, dst) in enumerate(
            [(g_in, g_ref), (m_in, m_ref), (v_in, v_ref), (r_in, r_ref), (k_in, k_ref), (group_in, group_ref)]
        )
    ]
    for copy in inputs:
        copy.start()

    def at(x_to, z_to, c_to):
        return ((x_to * Z + z_to) * C + c_to, y)

    def at_xc(to):
        return at(to // C, z, to % C)

    barrier = pltpu.get_barrier_semaphore()

    def greet(device):
        pl.semaphore_signal(barrier, inc=1, device_id=device, device_id_type=MESH)

    for d in FARTHEST_FIRST:
        greet(at(x, (z + d) % Z, c))
    for d in range(1, XC):
        greet(at_xc((xc + d) % XC))
    for d in range(1, Y):
        greet((me, (y + d) % Y))
    for copy in inputs:
        copy.wait()

    def prepare(i, carry):
        for k in range(4):
            row = i * 4 + k
            lanes = pl.ds(pl.multiple_of(row * LANES, LANES), LANES)
            u_own[:, lanes] = update_of(g_ref[:, lanes], m_ref[pl.ds(row, 1), :], v_ref[pl.ds(row, 1), :])
            seeds[lanes, :] = jnp.broadcast_to(r_ref[pl.ds(row, 1), :], (LANES, LANES)).T
        return carry

    lax.fori_loop(0, params // LANES // 4, prepare, 0)

    def chunk(update, depth, base, t):
        x_to, z_to = (x + 1 + t % X) % X, (z + 1 + t // X) % Z
        row = (x_to * Z + z_to) * C
        left, right = k_ref[pl.ds(row, 1), :], k_ref[pl.ds(row + 1, 1), :]
        strips = []
        for p in range(0, depth, 16):
            seed = seeds[pl.ds(pl.multiple_of(base + p, 16), 16), :]
            strips.append(jnp.concatenate([signs_of(seed * left), signs_of(seed * right)], axis=1))
        return jnp.dot(update, jnp.concatenate(strips, axis=0), preferred_element_type=F32)

    alone = Sums(
        0, at, x, z, c,
        (part_a, chip_a, sum_a, cols_a, rows_a, got_a), (cs_a, cr_a, xs_a, xr_a, zs_a, zr_a),
    )
    both = Sums(
        ALONE, at, x, z, c,
        (part_b, chip_b, sum_b, cols_b, rows_b, got_b), (cs_b, cr_b, xs_b, xr_b, zs_b, zr_b),
    )
    exchange = send(
        g_ref.at[:, pl.ds(pl.multiple_of((1 - side) * half, half), half)], g_other, gs.at[0], gr.at[0], partner
    )

    def pair_alone(i, carry):
        t = 2 * i
        alone.put(t, chunk(u_own[...], params, 0, t))
        alone.put(t + 1, chunk(u_own[...], params, 0, t + 1))

        @pl.when(i == 0)
        def _():
            pl.semaphore_wait(barrier, (XC - 1) + (Z - 1) + (Y - 1))
            exchange.start()

        alone.chip_copy(t).start()
        alone.chip_copy(t + 1).start()

        @pl.when(i >= 1)
        def _():
            alone.after_chip(t - 2)
            alone.after_chip(t - 1)

        @pl.when((t % X == 0) & (t >= 2 * X))
        def _():
            alone.after_x(t // X - 2)
            alone.z_copy(t // X - 2).start()

        return carry

    lax.fori_loop(0, ALONE * X // 2, pair_alone, 0)

    u_both[side] = u_own[:, pl.ds(pl.multiple_of(side * half, half), half)]
    exchange.wait_recv()

    def prepare_other(i, carry):
        for k in range(4):
            lanes = pl.ds(pl.multiple_of((i * 4 + k) * LANES, LANES), LANES)
            row = side * (half // LANES) + i * 4 + k
            u_both[1 - side, :, lanes] = update_of(g_other[:, lanes], m_ref[pl.ds(row, 1), :], v_ref[pl.ds(row, 1), :])
        return carry

    lax.fori_loop(0, half // LANES // 4, prepare_other, 0)

    def chunk_both(t):
        both.put(t, chunk(u_both[...].reshape(2 * examples, half), half, side * half, t))

    def pair_both(i, carry):
        t = ALONE * X + 2 * i
        chunk_both(t)
        chunk_both(t + 1)
        both.chip_copy(t).start()
        both.chip_copy(t + 1).start()

        @pl.when(i == 0)
        def _():
            alone.after_chip(ALONE * X - 2)
            alone.after_chip(ALONE * X - 1)
            alone.after_x(ALONE - 2)
            alone.z_copy(ALONE - 2).start()

        @pl.when(i == 3)
        def _():
            alone.after_x(ALONE - 1)
            alone.z_copy(ALONE - 1).start()

        @pl.when(i >= 1)
        def _():
            both.after_chip(t - 2)
            both.after_chip(t - 1)

        @pl.when((i % 2 == 1) & (i >= 5))
        def _():
            group = ALONE + (i - 5) // 2
            both.after_x(group)
            both.z_copy(group).start()

        return carry

    def step_both(t, carry):
        chunk_both(t)
        both.chip_copy(t).start()
        both.after_chip(t - 2)

        @pl.when(t == LAST - 1)
        def _():
            both.after_x(Z - 3)
            both.z_copy(Z - 3).start()

        return carry

    lax.fori_loop(0, (Z - 1 - ALONE) * X // 2, pair_both, 0)
    lax.fori_loop((Z - 1) * X, Z * X, step_both, 0)
    both.after_chip(LAST - 1)
    both.after_x(Z - 2)
    both.z_copy(Z - 2).start()
    both.after_chip(LAST)
    own = jnp.zeros((examples, LANES), F32)
    for group in range(ALONE):
        alone.z_copy(group).wait_recv()
        own = own + got_a[group]
    both.after_x(Z - 1)
    pair = rows_b[Z - 1 - ALONE]
    for group in range(ALONE, Z - 1):
        both.z_copy(group).wait_recv()
        pair = pair + got_b[group - ALONE]

    ybuf[y] = pair.reshape(2, examples, LANES)
    ybuf[y, side] = ybuf[y, side] + own

    def y_copy(d):
        return send(ybuf.at[y], ybuf.at[y], ys.at[d - 1], yr.at[d - 1], (me, (y + d) % Y))

    for d in range(1, Y):
        y_copy(d).start()
    exchange.wait_send()
    alone.sent(ALONE)
    both.sent(Z)
    for d in range(1, Y):
        y_copy(d).wait_recv()
    for e in range(Y):
        blocks[e] = ybuf[e, e % 2] + ybuf[e + 1 - 2 * (e % 2), e % 2]
    total = blocks[y]
    every = blocks[...].reshape(Y * examples, LANES)

    products = contract(total, every)
    squares = contract(jnp.ones((8, LANES), F32), every * every)
    for h in range(2):
        norm1[h : h + 1, :] = squares[:1, h * LANES : (h + 1) * LANES]
    for j in range(XC):
        send1[j] = products[j * Z : (j + 1) * Z, :]

    def send1_copies(d):
        to = (xc + d) % XC
        return (
            send(norm1, norm_recv.at[d - 1], n1s.at[d - 1], n1r.at[d - 1], at_xc(to)),
            send(send1.at[to], recv1.at[d - 1], s1s.at[d - 1], s1r.at[d - 1], at_xc(to)),
        )

    for d in range(1, XC):
        for copy in send1_copies(d):
            copy.start()
    for d in range(1, Y):
        y_copy(d).wait_send()
    block, norm = send1[xc], norm1[...]
    for d in range(1, XC):
        for copy in send1_copies(d):
            copy.wait_recv()
        block, norm = block + recv1[d - 1], norm + norm_recv[d - 1]
    planes[z] = block
    norm_planes[z] = norm

    def plane_copies(d):
        to = at(x, (z + d) % Z, c)
        return (
            send(norm_planes.at[z], norm_planes.at[z], n2s.at[d - 1], n2r.at[d - 1], to),
            send(planes.at[z], planes.at[z], s2s.at[d - 1], s2r.at[d - 1], to),
        )

    for d in FARTHEST_FIRST:
        for copy in plane_copies(d):
            copy.start()
    for d in range(1, XC):
        for copy in send1_copies(d):
            copy.wait_send()
    for d in range(1, Z):
        for copy in plane_copies(d):
            copy.wait_recv()
    block, norm = planes[0], norm_planes[0]
    for j in range(1, Z):
        block, norm = block + planes[j], norm + norm_planes[j]

    root_mean = jnp.sqrt(norm / features + 1e-06)
    example = y * examples + xc * Z + lax.broadcasted_iota(jnp.int32, (Z, LANES), 0)
    lane = lax.broadcasted_iota(jnp.int32, (Z, LANES), 1)
    labels = lax.broadcasted_iota(jnp.int32, (LANES, LANES), 0)
    own_root = jnp.zeros((Z, 1), F32)
    score, count = jnp.zeros((Z, LANES), F32), jnp.zeros((Z, LANES), F32)
    for h in range(2):
        row = jnp.broadcast_to(root_mean[h : h + 1, :], (Z, LANES))
        own_root = own_root + jnp.sum(jnp.where(lane + h * LANES == example, row, 0.0), axis=1, keepdims=True)
        onehot = (labels == group_ref[h : h + 1, :]).astype(F32)
        score = score + contract(block[:, h * LANES : (h + 1) * LANES] / row, onehot)
        count = count + contract(jnp.ones((Z, LANES), F32), onehot)
    count = jnp.where(count == 0, 1.0, count)
    scored[xc] = score / own_root / (count * features)

    def score_copy(d):
        return send(scored.at[xc], scored.at[xc], o1s.at[d - 1], o1r.at[d - 1], at_xc((xc + d) % XC))

    for d in range(1, XC):
        score_copy(d).start()
    for d in range(1, Z):
        for copy in plane_copies(d):
            copy.wait_send()

    here = y * examples + lax.broadcasted_iota(jnp.int32, (examples, LANES), 0)
    lane = lax.broadcasted_iota(jnp.int32, (examples, LANES), 1)
    column = jnp.zeros((examples, 1), F32)
    for h in range(2):
        row = jnp.broadcast_to(root_mean[h : h + 1, :], (examples, LANES))
        column = column + jnp.sum(jnp.where(lane + h * LANES == here, row, 0.0), axis=1, keepdims=True)
    f_ref[...] = total / column

    for d in range(1, XC):
        score_copy(d).wait_recv()
    s_ref[...] = scored[...].reshape(examples, LANES)[:, :GROUPS]

    for d in range(1, XC):
        score_copy(d).wait_send()


def solution(mesh):
    def shards(gradients, m_state, v_state, row_seeds, col_seeds, group_of):
        examples, params = gradients.shape
        rows = (-1, LANES)
        dma, vmem = pltpu.SemaphoreType.DMA, pltpu.VMEM
        wide = Y * examples

        def buffers(groups, rows):
            block = (rows, LANES)
            return [
                vmem((groups * X, 2, *block), F32),
                vmem((groups * X, *block), F32),
                vmem((groups, X, *block), F32),
                vmem((groups, X, *block), F32),
                vmem((groups, *block), F32),
                vmem((groups, *block), F32),
            ]

        def semaphores(groups):
            return [
                dma((groups * X,)), dma((groups * X,)),
                dma((groups, X)), dma((groups, X)),
                dma((groups,)), dma((groups,)),
            ]

        arguments = [
            gradients, m_state.reshape(rows), v_state.reshape(rows), row_seeds.reshape(rows),
            col_seeds.reshape(rows), group_of.reshape(rows),
        ]
        return pl.pallas_call(
            kernel,
            out_shape=(
                jax.ShapeDtypeStruct((examples, LANES), F32),
                jax.ShapeDtypeStruct((examples, GROUPS), F32),
            ),
            in_specs=[pl.BlockSpec(memory_space=pltpu.HBM)] * 6,
            out_specs=[pl.BlockSpec(memory_space=pltpu.VMEM)] * 2,
            scratch_shapes=[
                *[vmem(array.shape, array.dtype) for array in arguments],
                dma((6,)),
                vmem((examples, params), jnp.bfloat16),
                vmem((2, examples, params // 2), jnp.bfloat16),
                vmem((examples, params // 2), F32),
                vmem((params, LANES), jnp.int32),
                *buffers(ALONE, examples),
                *buffers(Z - ALONE, 2 * examples),
                vmem((Y, 2, examples, LANES), F32),
                vmem((Y, examples, LANES), F32),
                vmem((XC, Z, wide), F32),
                vmem((XC - 1, Z, wide), F32),
                vmem((Z, Z, wide), F32),
                vmem((2, LANES), F32),
                vmem((XC - 1, 2, LANES), F32),
                vmem((Z, 2, LANES), F32),
                vmem((XC, Z, LANES), F32),
                dma((1,)), dma((1,)),
                *semaphores(ALONE),
                *semaphores(Z - ALONE),
                dma((Y - 1,)), dma((Y - 1,)),
                dma((XC - 1,)), dma((XC - 1,)),
                dma((Z - 1,)), dma((Z - 1,)),
                dma((XC - 1,)), dma((XC - 1,)),
                dma((Z - 1,)), dma((Z - 1,)),
                dma((XC - 1,)), dma((XC - 1,)),
            ],
            compiler_params=pltpu.CompilerParams(
                collective_id=0, has_side_effects=True, vmem_limit_bytes=48 << 20
            ),
            name="features_and_scores",
        )(*[pltpu.with_memory_space_constraint(array, pltpu.HBM) for array in arguments])

    in_specs = (P("ex", "param"), P("param"), P("param"), P("param"), P(), P())
    out_specs = (P("ex", "param"), P("ex", None))
    return jax.shard_map(shards, mesh=mesh, in_specs=in_specs, out_specs=out_specs, check_vma=False)
```
